32 devices in a mesh: row: 8 (over z, x), col: 4 (over y, core).
Axes of the slice: x: 2, y: 2, z: 4, core: 2. Of those that a mesh axis runs over, the one named last changes fastest.
Arguments:
- tokens: bfloat16 [2048, 8192], P('row', 'col'), may hold values from -6 to 6
- weight: bfloat16 [8192, 16384], P('col', 'row'), may hold values from -0.0625 to 0.0625
- grad: bfloat16 [8192, 16384], P('col', 'row'), may hold values from -0.0625 to 0.0625
- roots: bfloat16 [2, 8, 2, 16, 1024, 1024], P(None, 'col', None, 'row')
- owner: int32 [8, 16], replicated, may hold values from 0 to 7, as said below
Outputs:
- new_weight: bfloat16 [8192, 16384], P('col', 'row')
- output: bfloat16 [2048, 16384], P('col', 'row')
The draws below stay inside these ranges and needn't reach their ends.
Inputs may be any that keep to these rules, and one draw needn't show every extreme that they name: owner[p, q] is the block's home q // 2 or the next index (q // 2 + 1) mod 8; in every draw some index along row keeps the roots of all blocks of its own home and of the previous home.
All inputs are finite; a program needn't handle non-finite values.
Results may differ from the reference program's by a relative error of at most 0.013.
Values may be sent and summed in bfloat16 or wider, within the bound.
No kernel may reach another device: no remote copies, remote signals or barrier semaphores. Data moves between devices by JAX's collectives and lax.ppermute only.
A program may use at most 256 MiB of HBM per device.

```python
import math
import jax
import jax.numpy as jnp
from jax import lax

D = 8192
FF = 16384
BLK = 1024
TOKENS = 2048
FBLK = 2
N_ROW = 8
N_COL = 4


def draw_roots(key, part):
    noise_key = jax.random.fold_in(key, 11)
    scale_key = jax.random.fold_in(key, 12)
    shape = (2, D // BLK, 2, FF // BLK, BLK, BLK)
    spread = jax.random.normal(noise_key, shape, jnp.float32) * (0.6 / math.sqrt(BLK))
    levels = jnp.exp(jax.random.uniform(scale_key, shape[:-1], jnp.float32, math.log(0.5), math.log(2.0)))
    places = jnp.arange(BLK, dtype=jnp.int32)
    identity = (places[:, None] == places[None, :]).astype(jnp.float32)
    return (spread + identity * levels[..., None]).astype(jnp.bfloat16)


def draw_owner(key, part):
    offset_key = jax.random.fold_in(key, 21)
    busy_key = jax.random.fold_in(key, 22)
    per_home = FF // (N_ROW * BLK)
    offsets = jax.random.randint(offset_key, (D // BLK, FF // BLK), 0, 2, jnp.int32)
    busiest = jax.random.randint(busy_key, (), 0, N_ROW, jnp.int32)
    home = jnp.broadcast_to((jnp.arange(FF // BLK, dtype=jnp.int32) // per_home)[None, :], offsets.shape)
    offsets = jnp.where(home == busiest, 0, offsets)
    offsets = jnp.where(home == jnp.mod(busiest - 1 + N_ROW, N_ROW), 1, offsets)
    return jnp.mod(home + offsets, N_ROW).astype(jnp.int32)


def shard_levels(key, shape, split, smallest, largest):
    loudness = 1.0
    for dim, shards_of in split:
        heights = jax.random.uniform(jax.random.fold_in(jax.random.fold_in(key, 6), dim), (shards_of,), jnp.float32, smallest / len(split), largest / len(split))
        loudness = loudness * jnp.repeat(jnp.exp(heights), shape[dim] // shards_of).reshape((-1,) + (1,) * (len(shape) - 1 - dim))
    return loudness


def bell_draw(key, extent, width, reach, split=(), held_as=jnp.bfloat16):
    level = shard_levels(key, extent, split, -0.22, 0.18) if split else 1.0
    result = jax.random.normal(key, extent, jnp.float32) * width * level
    return jnp.minimum(jnp.maximum(result, -reach), reach).astype(held_as)


def setup_inputs(seed: int = 0) -> dict:
    seeds = jax.random.split(jax.random.key(seed), 6)
    return {
        "tokens": bell_draw(seeds[0], (TOKENS, D), 1.0, 6.0, ((0, 8), (1, 4))),
        "weight": bell_draw(seeds[1], (D, FF), D ** -0.5, 0.0625, ((0, 4), (1, 8))),
        "grad": bell_draw(seeds[2], (D, FF), D ** -0.5, 0.0625, ((0, 4), (1, 8))),
        "roots": draw_roots(jax.random.fold_in(seeds[5], 71), 0),
        "owner": draw_owner(jax.random.fold_in(seeds[5], 71), 0),
    }


step_size = 0.5


def reference(tokens, weight, grad, roots, owner):
    down_blocks = D // BLK
    across_blocks = FF // BLK
    home = (jnp.arange(across_blocks, dtype=jnp.int32) // FBLK).astype(jnp.int32)

    def row_block(index):
        start = (index * BLK).astype(jnp.int32)
        grad_rows = lax.dynamic_slice_in_dim(grad, start, BLK, 0).reshape(BLK, across_blocks, BLK).transpose(1, 0, 2)
        weight_rows = lax.dynamic_slice_in_dim(weight, start, BLK, 0).reshape(BLK, across_blocks, BLK).transpose(1, 0, 2)
        slab = roots[:, index]
        at_home = (owner[index] == home)[:, None, None]
        left_root = jnp.where(at_home, slab[0, 0], jnp.roll(slab[0, 1], -FBLK, axis=0))
        right_root = jnp.where(at_home, slab[1, 0], jnp.roll(slab[1, 1], -FBLK, axis=0))
        mixed = jnp.einsum("qab,qbc->qac", left_root.astype(jnp.float32), grad_rows.astype(jnp.float32)).astype(jnp.bfloat16)
        update = jnp.einsum("qab,qbc->qac", mixed.astype(jnp.float32), right_root.astype(jnp.float32))
        fresh = (weight_rows.astype(jnp.float32) - step_size * update).astype(jnp.bfloat16)
        return fresh.transpose(1, 0, 2).reshape(BLK, FF)

    new_weight = lax.map(row_block, jnp.arange(down_blocks, dtype=jnp.int32)).reshape(D, FF)
    slice_width = D // N_COL

    def add_term(total, index):
        start = (index * slice_width).astype(jnp.int32)
        inputs = lax.dynamic_slice_in_dim(tokens, start, slice_width, 1)
        rows = lax.dynamic_slice_in_dim(new_weight, start, slice_width, 0)
        part = lax.optimization_barrier(jnp.dot(inputs, rows, preferred_element_type=jnp.float32).astype(jnp.bfloat16))
        return total + part.astype(jnp.float32), None

    total, unused = lax.scan(add_term, jnp.zeros((TOKENS, FF), jnp.float32), jnp.arange(N_COL, dtype=jnp.int32))
    return new_weight, total.astype(jnp.bfloat16)
```

```python
import jax
import jax.numpy as jnp
from jax import lax
from jax.experimental import pallas as pl
from jax.experimental.pallas import tpu as pltpu
from jax.sharding import PartitionSpec as P

step_size = 0.5


def shift_route(count, distance):
    return [(i, (i + distance) % count) for i in range(count)]


def pair_route(count):
    return [(i, i ^ 1) for i in range(count)]


def after(value, *others):
    return lax.optimization_barrier((value,) + others)[0]


def precondition(flags, roots, slot, q, grads, grads_q, kind):
    width = roots.shape[-1]
    down = grads.shape[0] // width
    tile = min(width, 256)

    def kernel(flag_ref, left_ref, grad_ref, right_ref, out_ref):
        @pl.when(flag_ref[pl.program_id(0)] != 0)
        def _():
            @pl.loop(0, width // tile)
            def _(i):
                rows = pl.ds(pl.multiple_of(i * tile, tile), tile)
                mixed = jnp.dot(left_ref[rows, :], grad_ref[...], preferred_element_type=jnp.float32)
                update = jnp.dot(mixed.astype(jnp.bfloat16), right_ref[...], preferred_element_type=jnp.float32)
                out_ref[rows, :] = update.astype(kind)

        @pl.when(flag_ref[pl.program_id(0)] == 0)
        def _():
            out_ref[...] = jnp.zeros_like(out_ref)

    def root_spec(side):
        return pl.BlockSpec((None, None, None, None, width, width), lambda p, f: (side, p, slot, q, 0, 0))

    size = 2 if kind == jnp.bfloat16 else 4
    return pl.pallas_call(
        kernel,
        out_shape=jax.ShapeDtypeStruct((down * width, width), kind),
        grid_spec=pltpu.PrefetchScalarGridSpec(
            num_scalar_prefetch=1,
            grid=(down,),
            in_specs=[root_spec(0), pl.BlockSpec((width, width), lambda p, f: (p, grads_q)), root_spec(1)],
            out_specs=pl.BlockSpec((width, width), lambda p, f: (p, 0)),
        ),
        compiler_params=pltpu.CompilerParams(vmem_limit_bytes=40 << 20),
        cost_estimate=pl.CostEstimate(
            flops=down * 4 * width**3, bytes_accessed=down * width * width * (6 + size), transcendentals=0
        ),
        name="precondition",
    )(flags, roots, grads, roots)


def gather_tokens(tokens, row_count, row_place):
    rows = tokens.shape[0]
    other = lax.ppermute(tokens, "row", pair_route(row_count))
    low = jnp.mod(row_place, 2) == 0
    pair = jnp.concatenate([jnp.where(low, tokens, other), jnp.where(low, other, tokens)], axis=0)
    pairs = row_count // 2
    place = row_place // 2
    gathered = jnp.zeros((rows * row_count, tokens.shape[1]), tokens.dtype)

    def put(whole, piece, index):
        return lax.dynamic_update_slice(whole, piece, (jnp.mod(index, pairs) * (2 * rows), 0))

    gathered = put(gathered, pair, place)
    up = below = pair
    for step in range(1, pairs // 2 + 1):
        up = lax.ppermute(up, "row", shift_route(row_count, 2))
        gathered = put(gathered, up, place - step)
        if step <= (pairs - 1) // 2:
            below = lax.ppermute(below, "row", shift_route(row_count, -2))
            gathered = put(gathered, below, place + step)
    return gathered


def pair_sum(terms, col_count, col_place):
    rows = terms.shape[0] // col_count
    terms = terms.reshape(col_count // 2, 2, rows, terms.shape[1])
    core = jnp.mod(col_place, 2)
    mine = lax.dynamic_index_in_dim(terms, core, 1, keepdims=False)
    others = lax.dynamic_index_in_dim(terms, 1 - core, 1, keepdims=False)
    came = lax.ppermute(others, "col", pair_route(col_count))
    return mine.astype(jnp.float32) + came.astype(jnp.float32)


def far_sum(halves, col_count, col_place):
    groups = col_count // 2
    place = col_place // 2
    total = lax.dynamic_index_in_dim(halves, place, 0, keepdims=False)
    sent = halves.astype(jnp.bfloat16)
    for step in range(1, groups):
        piece = lax.dynamic_index_in_dim(sent, jnp.mod(place + step, groups), 0, keepdims=False)
        total = total + lax.ppermute(piece, "col", shift_route(col_count, 2 * step)).astype(jnp.float32)
    return total.astype(jnp.bfloat16)


def on_device(tokens, weight, grad, roots, owner):
    width = roots.shape[-1]
    down = weight.shape[0] // width
    across = weight.shape[1] // width
    row_place = lax.axis_index("row")
    col_place = lax.axis_index("col")
    row_count = lax.axis_size("row")
    col_count = lax.axis_size("col")
    previous = jnp.mod(row_place - 1 + row_count, row_count)
    own_owner = lax.dynamic_slice(owner, (col_place * down, row_place * across), (down, across))
    prior_owner = lax.dynamic_slice(owner, (col_place * down, previous * across), (down, across))
    kept = (own_owner == row_place).astype(jnp.int32)
    taken = (prior_owner == row_place).astype(jnp.int32)
    forth = shift_route(row_count, 1)
    back = shift_route(row_count, -1)

    came = []
    for q in range(across):
        column = grad[:, q * width:(q + 1) * width]
        came.append(lax.ppermute(column if q == 0 else after(column, came[q - 1]), "row", forth))
    all_tokens = gather_tokens(tokens, row_count, row_place)

    new_weight = jnp.zeros_like(weight)
    output = jnp.zeros((all_tokens.shape[0] // col_count, weight.shape[1]), jnp.bfloat16)
    returned = []
    homes = []
    for q in range(across):
        flags = kept[:, q] if q == 0 else after(kept[:, q], lent)
        homes.append(precondition(flags, roots, 0, q, grad, q, jnp.float32))
        lent = precondition(taken[:, q], roots, 1, q, after(came[q], homes[q]) if q == 0 else came[q], 0, jnp.bfloat16)
        cuts = [0, width] if q < across - 1 else [0, width // 2, width * 3 // 4, width]
        last = None
        for start, stop in zip(cuts[:-1], cuts[1:]):
            piece = lent[:, start:stop]
            if last is not None:
                piece = after(piece, last)
            last = lax.ppermute(piece, "row", back)
            returned.append((q, start, stop, last))
    gate = None
    for q, start, stop, piece in returned:
        if gate is not None:
            piece = after(piece, gate)
        at = q * width + start
        flags = jnp.repeat(kept[:, q] != 0, width)[:, None]
        update = jnp.where(flags, homes[q][:, start:stop], piece.astype(jnp.float32))
        fresh = (weight[:, at:at + stop - start].astype(jnp.float32) - step_size * update).astype(jnp.bfloat16)
        new_weight = lax.dynamic_update_slice(new_weight, fresh, (0, at))
        terms = jnp.dot(all_tokens, fresh, preferred_element_type=jnp.float32).astype(jnp.bfloat16)
        halves = pair_sum(terms, col_count, col_place)
        gate = halves
        output = lax.dynamic_update_slice(output, far_sum(halves, col_count, col_place), (0, at))
    return new_weight, output


def solution(mesh):
    placed = (
        P("row", "col"),
        P("col", "row"),
        P("col", "row"),
        P(None, "col", None, "row", None, None),
        P(),
    )
    return jax.shard_map(
        on_device,
        mesh=mesh,
        in_specs=placed,
        out_specs=(P("col", "row"), P("col", "row")),
        check_vma=False,
    )
```

```python
import jax
import jax.numpy as jnp
from jax import lax
from jax.experimental import pallas as pl
from jax.experimental.pallas import tpu as pltpu
from jax.sharding import PartitionSpec as P

step_size = 0.5


def shift_route(count, distance):
    return [(i, (i + distance) % count) for i in range(count)]


def pair_route(count):
    return [(i, i ^ 1) for i in range(count)]


def together(*values):
    return lax.optimization_barrier(values)


def root_spec(roots, side, slot, block):
    width = roots.shape[-1]
    return pl.BlockSpec((None, None, None, None, width, width), lambda *at: (side, block(*at)[0], slot, block(*at)[1], 0, 0))


def update_rows(left_ref, grad_ref, right_ref, rows):
    mixed = jnp.dot(left_ref[rows, :], grad_ref[...], preferred_element_type=jnp.float32)
    return jnp.dot(mixed.astype(jnp.bfloat16), right_ref[...], preferred_element_type=jnp.float32)


def cost(blocks, width, arrays):
    return pl.CostEstimate(
        flops=blocks * 4 * width**3, bytes_accessed=blocks * 2 * arrays * width * width, transcendentals=0
    )


def precondition_lent(flags, roots, q, came, cuts, later_than):
    width = roots.shape[-1]
    down = came.shape[0] // width
    tile = min(width, 256)
    pieces = list(zip(cuts[:-1], cuts[1:]))

    def kernel(flag_ref, left_ref, grad_ref, right_ref, *rest):
        *out_refs, mark_ref = rest[-len(pieces) - 1:]
        mark_ref[...] = jnp.zeros_like(mark_ref)

        @pl.when(flag_ref[pl.program_id(0)] != 0)
        def _():
            @pl.loop(0, width // tile)
            def _(i):
                rows = pl.ds(pl.multiple_of(i * tile, tile), tile)
                update = update_rows(left_ref, grad_ref, right_ref, rows).astype(jnp.bfloat16)
                for (start, stop), out_ref in zip(pieces, out_refs):
                    out_ref[rows, :] = update[:, start:stop]

        @pl.when(flag_ref[pl.program_id(0)] == 0)
        def _():
            for out_ref in out_refs:
                out_ref[...] = jnp.zeros_like(out_ref)

    return pl.pallas_call(
        kernel,
        out_shape=[jax.ShapeDtypeStruct((down * width, stop - start), jnp.bfloat16) for start, stop in pieces]
        + [jax.ShapeDtypeStruct((8, 128), jnp.float32)],
        grid_spec=pltpu.PrefetchScalarGridSpec(
            num_scalar_prefetch=1,
            grid=(down,),
            in_specs=[
                root_spec(roots, 0, 1, lambda p, f: (p, q)),
                pl.BlockSpec((width, width), lambda p, f: (p, q)),
                root_spec(roots, 1, 1, lambda p, f: (p, q)),
            ]
            + [pl.BlockSpec(memory_space=pl.ANY)] * len(later_than),
            out_specs=[pl.BlockSpec((width, stop - start), lambda p, f: (p, 0)) for start, stop in pieces]
            + [pl.BlockSpec((8, 128), lambda p, f: (0, 0))],
        ),
        compiler_params=pltpu.CompilerParams(vmem_limit_bytes=40 << 20),
        cost_estimate=cost(down, width, 4),
        name="precondition_lent",
    )(flags, roots, came, roots, *later_than)


def precondition_home(kept_column, roots, grad, weight, q, new_weight, later_than):
    width = roots.shape[-1]
    down = kept_column.shape[0]
    tile = min(width, 256)

    def kernel(flag_ref, left_ref, grad_ref, right_ref, weight_ref, *rest):
        out_ref = rest[-1]

        @pl.when(flag_ref[pl.program_id(0)] != 0)
        def _():
            @pl.loop(0, width // tile)
            def _(i):
                rows = pl.ds(pl.multiple_of(i * tile, tile), tile)
                update = update_rows(left_ref, grad_ref, right_ref, rows)
                out_ref[rows, :] = (weight_ref[rows, :].astype(jnp.float32) - step_size * update).astype(jnp.bfloat16)

        @pl.when(flag_ref[pl.program_id(0)] == 0)
        def _():
            out_ref[...] = weight_ref[...]

    tiles = pl.BlockSpec((width, width), lambda p, f: (p, q))
    extra = ([] if new_weight is None else [new_weight]) + list(later_than)
    return pl.pallas_call(
        kernel,
        out_shape=jax.ShapeDtypeStruct(weight.shape, jnp.bfloat16),
        grid_spec=pltpu.PrefetchScalarGridSpec(
            num_scalar_prefetch=1,
            grid=(down,),
            in_specs=[
                root_spec(roots, 0, 0, lambda p, f: (p, q)),
                tiles,
                root_spec(roots, 1, 0, lambda p, f: (p, q)),
                tiles,
            ]
            + [pl.BlockSpec(memory_space=pl.ANY)] * len(extra),
            out_specs=tiles,
        ),
        input_output_aliases={} if new_weight is None else {5: 0},
        compiler_params=pltpu.CompilerParams(vmem_limit_bytes=48 << 20),
        cost_estimate=cost(down, width, 5),
        name="precondition_home",
    )(kept_column, roots, grad, roots, weight, *extra)


def finish_columns(flags, down, across, q, col_count, new_weight, piece, tokens, start, width, later_than):
    depth = piece.shape[0]
    at = (q * piece.shape[1] + start) // width
    height = depth // down
    rows = tokens.shape[0] // col_count
    half = col_count // 2
    tile = min(width, 256)

    def kernel(flag_ref, weight_ref, piece_ref, token_ref, *rest):
        new_ref, others_ref, mine_ref = rest[-3:]
        step = pl.program_id(0)

        @pl.when(step == 0)
        def _():
            for p in range(down):
                own = slice(p * height, (p + 1) * height)

                @pl.when(flag_ref[p * across + q] != 0)
                def _():
                    new_ref[own, :] = weight_ref[own, :]

                @pl.when(flag_ref[p * across + q] == 0)
                def _():
                    update = step_size * piece_ref[own, :].astype(jnp.float32)
                    new_ref[own, :] = (weight_ref[own, :].astype(jnp.float32) - update).astype(jnp.bfloat16)

        def product(out_ref):
            @pl.loop(0, width // tile)
            def _(i):
                some = pl.ds(pl.multiple_of(i * tile, tile), tile)
                term = jnp.dot(token_ref[...], new_ref[:, some], preferred_element_type=jnp.float32)
                out_ref[:, some] = term.astype(jnp.bfloat16)

        @pl.when(step < half)
        def _():
            product(others_ref)

        @pl.when(step >= half)
        def _():
            product(mine_ref)

    def chunk(t, f):
        core = f[down * across]
        return jnp.where(t < half, 2 * t + 1 - core, 2 * (t - half) + core)

    columns = pl.BlockSpec((depth, width), lambda t, f: (0, at))
    terms = jax.ShapeDtypeStruct((half, rows, width), jnp.bfloat16)
    return pl.pallas_call(
        kernel,
        out_shape=(jax.ShapeDtypeStruct(new_weight.shape, jnp.bfloat16), terms, terms),
        grid_spec=pltpu.PrefetchScalarGridSpec(
            num_scalar_prefetch=1,
            grid=(col_count,),
            in_specs=[
                columns,
                pl.BlockSpec((depth, width), lambda t, f: (0, start // width)),
                pl.BlockSpec((rows, depth), lambda t, f: (chunk(t, f), 0)),
            ]
            + [pl.BlockSpec(memory_space=pl.ANY)] * len(later_than),
            out_specs=(
                columns,
                pl.BlockSpec((None, rows, width), lambda t, f: (jnp.minimum(t, half - 1), 0, 0)),
                pl.BlockSpec((None, rows, width), lambda t, f: (jnp.maximum(t - half, 0), 0, 0)),
            ),
        ),
        input_output_aliases={1: 0},
        compiler_params=pltpu.CompilerParams(vmem_limit_bytes=56 << 20),
        cost_estimate=pl.CostEstimate(flops=1000, bytes_accessed=1000, transcendentals=0),
        name="finish_columns",
    )(flags, new_weight, piece, tokens, *later_than)


def swap_tokens(tokens, row_count, row_place):
    other = lax.ppermute(tokens, "row", pair_route(row_count))
    low = jnp.mod(row_place, 2) == 0
    return jnp.concatenate([jnp.where(low, tokens, other), jnp.where(low, other, tokens)], axis=0)


def ring_direct(pair, row_count, side):
    sides = range(side, row_count, 2)
    return [
        lax.ppermute(pair, "row", [(i, (i + 2 * step) % row_count) for i in sides])
        for step in range(1, row_count // 2)
    ]


def line_step(up, down, row_count, side):
    ups = lax.ppermute(up, "row", [(i, i + 2) for i in range(side, row_count - 2, 2)])
    downs = lax.ppermute(down, "row", [(i + 2, i) for i in range(side, row_count - 2, 2)])
    return ups, downs


def put_pairs(pair, early, late, row_place):
    pairs = len(early) + 1
    rows, depth = pair.shape
    ups = [up for up, _ in late]
    downs = [below for _, below in late]

    def kernel(place_ref, *refs):
        pair_ref, *others, out_ref, sem = refs
        early_refs, up_refs, down_refs = (others[i * (pairs - 1):(i + 1) * (pairs - 1)] for i in range(3))
        t = pl.program_id(0)
        apart = place_ref[0] - t
        odd = place_ref[1] == 1
        cases = [(apart == 0, pair_ref)]
        for step in range(1, pairs):
            cases.append((jnp.logical_and(odd, apart == step), up_refs[step - 1]))
            cases.append((jnp.logical_and(odd, apart == -step), down_refs[step - 1]))
            around = jnp.logical_or(apart == step, apart == step - pairs)
            cases.append((jnp.logical_and(jnp.logical_not(odd), around), early_refs[step - 1]))
        for case, source in cases:
            @pl.when(case)
            def _():
                copy = pltpu.make_async_copy(source, out_ref, sem)
                copy.start()
                copy.wait()

    count = 1 + 3 * (pairs - 1)
    return pl.pallas_call(
        kernel,
        out_shape=jax.ShapeDtypeStruct((rows * pairs, depth), pair.dtype),
        grid_spec=pltpu.PrefetchScalarGridSpec(
            num_scalar_prefetch=1,
            grid=(pairs,),
            in_specs=[pl.BlockSpec(memory_space=pl.ANY)] * count,
            out_specs=pl.BlockSpec((rows, depth), lambda t, f: (t, 0)),
            scratch_shapes=[pltpu.SemaphoreType.DMA],
        ),
        cost_estimate=pl.CostEstimate(flops=1000, bytes_accessed=1000, transcendentals=0),
        name="put_pairs",
    )(jnp.stack([row_place // 2, row_place % 2]), pair, *early, *ups, *downs)


def far_sum(mine, came, col_count, col_place):
    halves = mine.astype(jnp.float32) + came.astype(jnp.float32)
    groups = col_count // 2
    place = col_place // 2
    total = lax.dynamic_index_in_dim(halves, place, 0, keepdims=False)
    sent = halves.astype(jnp.bfloat16)
    for step in range(1, groups):
        piece = lax.dynamic_index_in_dim(sent, jnp.mod(place + step, groups), 0, keepdims=False)
        total = total + lax.ppermute(piece, "col", shift_route(col_count, 2 * step)).astype(jnp.float32)
    return total.astype(jnp.bfloat16)


def on_device(tokens, weight, grad, roots, owner):
    width = roots.shape[-1]
    down = weight.shape[0] // width
    across = weight.shape[1] // width
    row_place = lax.axis_index("row")
    col_place = lax.axis_index("col")
    row_count = lax.axis_size("row")
    col_count = lax.axis_size("col")
    previous = jnp.mod(row_place - 1 + row_count, row_count)
    own_owner = lax.dynamic_slice(owner, (col_place * down, row_place * across), (down, across))
    prior_owner = lax.dynamic_slice(owner, (col_place * down, previous * across), (down, across))
    kept = (own_owner == row_place).astype(jnp.int32)
    taken = (prior_owner == row_place).astype(jnp.int32)
    forth = shift_route(row_count, 1)
    back = shift_route(row_count, -1)

    swapped = swap_tokens(tokens, row_count, row_place)
    swapped, grad = together(swapped, grad)
    came = lax.ppermute(grad, "row", forth)
    early = ring_direct(swapped, row_count, 0)
    came, late_pair, *early = together(came, swapped, *early)

    returned = []
    new_weight = None
    for q in range(across):
        later_than = () if new_weight is None else (new_weight,)
        lent, mark = precondition_lent(taken[:, q], roots, q, came, (0, width), later_than)
        returned.append(lax.ppermute(lent, "row", back))
        new_weight = precondition_home(kept[:, q], roots, grad, weight, q, new_weight, (mark,))

    late = []
    up = down_piece = late_pair
    first_piece = returned[0]
    for step in range(1, row_count // 2):
        if step == row_count // 2 - 1:
            up, down_piece, first_piece, new_weight = together(up, down_piece, first_piece, new_weight)
        up, down_piece = line_step(up, down_piece, row_count, 1)
        late.append((up, down_piece))
    returned[0] = first_piece
    all_tokens = put_pairs(swapped, early, late, row_place)
    output = jnp.zeros((all_tokens.shape[0] // col_count, weight.shape[1]), jnp.bfloat16)

    flags = jnp.concatenate([kept.reshape(-1), jnp.mod(col_place, 2).reshape(1)])

    half = width // 2
    parts = [(q, 0, width) for q in range(across - 1)] + [(across - 1, 0, half), (across - 1, half, half)]
    later_than = ()
    ahead = ()
    for k, (q, start, size) in enumerate(parts):
        if k == len(parts) - 1:
            later_than = later_than + ahead
        new_weight, others, mine = finish_columns(
            flags, down, across, q, col_count, new_weight, returned[q], all_tokens, start, size, later_than
        )
        other = lax.ppermute(others, "col", pair_route(col_count))
        total = far_sum(mine, other, col_count, col_place)
        output = lax.dynamic_update_slice(output, total, (0, q * width + start))
        later_than = (mine,)
        if q < across - 1:
            ahead = ahead + (total,)
    return new_weight, output


def solution(mesh):
    placed = (
        P("row", "col"),
        P("col", "row"),
        P("col", "row"),
        P(None, "col", None, "row", None, None),
        P(),
    )
    return jax.shard_map(
        on_device,
        mesh=mesh,
        in_specs=placed,
        out_specs=(P("col", "row"), P("col", "row")),
        check_vma=False,
    )
```

```python
import jax
import jax.numpy as jnp
from jax import lax
from jax.experimental import pallas as pl
from jax.experimental.pallas import tpu as pltpu
from jax.sharding import PartitionSpec as P

step_size = 0.5


def shift_route(count, distance):
    return [(i, (i + distance) % count) for i in range(count)]


def pair_route(count):
    return [(i, i ^ 1) for i in range(count)]


def together(*values):
    return lax.optimization_barrier(values)


def root_spec(roots, side, slot, block):
    width = roots.shape[-1]
    return pl.BlockSpec((None, None, None, None, width, width), lambda *at: (side, block(*at)[0], slot, block(*at)[1], 0, 0))


def update_rows(left_ref, grad_ref, right_ref, rows):
    mixed = jnp.dot(left_ref[rows, :], grad_ref[...], preferred_element_type=jnp.float32)
    return jnp.dot(mixed.astype(jnp.bfloat16), right_ref[...], preferred_element_type=jnp.float32)


def cost(blocks, width, arrays):
    return pl.CostEstimate(
        flops=blocks * 4 * width**3, bytes_accessed=blocks * 2 * arrays * width * width, transcendentals=0
    )


def precondition_lent(flags, roots, q, came, cuts, later_than):
    width = roots.shape[-1]
    down = came.shape[0] // width
    tile = min(width, 256)
    pieces = list(zip(cuts[:-1], cuts[1:]))

    def kernel(flag_ref, left_ref, grad_ref, right_ref, *rest):
        *out_refs, mark_ref = rest[-len(pieces) - 1:]
        mark_ref[...] = jnp.zeros_like(mark_ref)

        @pl.when(flag_ref[pl.program_id(0)] != 0)
        def _():
            @pl.loop(0, width // tile)
            def _(i):
                rows = pl.ds(pl.multiple_of(i * tile, tile), tile)
                update = update_rows(left_ref, grad_ref, right_ref, rows).astype(jnp.bfloat16)
                for (start, stop), out_ref in zip(pieces, out_refs):
                    out_ref[rows, :] = update[:, start:stop]

        @pl.when(flag_ref[pl.program_id(0)] == 0)
        def _():
            for out_ref in out_refs:
                out_ref[...] = jnp.zeros_like(out_ref)

    return pl.pallas_call(
        kernel,
        out_shape=[jax.ShapeDtypeStruct((down * width, stop - start), jnp.bfloat16) for start, stop in pieces]
        + [jax.ShapeDtypeStruct((8, 128), jnp.float32)],
        grid_spec=pltpu.PrefetchScalarGridSpec(
            num_scalar_prefetch=1,
            grid=(down,),
            in_specs=[
                root_spec(roots, 0, 1, lambda p, f: (p, q)),
                pl.BlockSpec((width, width), lambda p, f: (p, q)),
                root_spec(roots, 1, 1, lambda p, f: (p, q)),
            ]
            + [pl.BlockSpec(memory_space=pl.ANY)] * len(later_than),
            out_specs=[pl.BlockSpec((width, stop - start), lambda p, f: (p, 0)) for start, stop in pieces]
            + [pl.BlockSpec((8, 128), lambda p, f: (0, 0))],
        ),
        compiler_params=pltpu.CompilerParams(vmem_limit_bytes=60 << 20),
        cost_estimate=cost(down, width, 4),
        name="precondition_lent",
    )(flags, roots, came, roots, *later_than)


def precondition_home(kept_column, roots, grad, weight, q, new_weight, later_than):
    width = roots.shape[-1]
    down = kept_column.shape[0]
    tile = min(width, 256)

    def kernel(flag_ref, left_ref, grad_ref, right_ref, weight_ref, *rest):
        out_ref = rest[-1]

        @pl.when(flag_ref[pl.program_id(0)] != 0)
        def _():
            @pl.loop(0, width // tile)
            def _(i):
                rows = pl.ds(pl.multiple_of(i * tile, tile), tile)
                update = update_rows(left_ref, grad_ref, right_ref, rows)
                out_ref[rows, :] = (weight_ref[rows, :].astype(jnp.float32) - step_size * update).astype(jnp.bfloat16)

        @pl.when(flag_ref[pl.program_id(0)] == 0)
        def _():
            out_ref[...] = weight_ref[...]

    tiles = pl.BlockSpec((width, width), lambda p, f: (p, q))
    extra = ([] if new_weight is None else [new_weight]) + list(later_than)
    return pl.pallas_call(
        kernel,
        out_shape=jax.ShapeDtypeStruct(weight.shape, jnp.bfloat16),
        grid_spec=pltpu.PrefetchScalarGridSpec(
            num_scalar_prefetch=1,
            grid=(down,),
            in_specs=[
                root_spec(roots, 0, 0, lambda p, f: (p, q)),
                tiles,
                root_spec(roots, 1, 0, lambda p, f: (p, q)),
                tiles,
            ]
            + [pl.BlockSpec(memory_space=pl.ANY)] * len(extra),
            out_specs=tiles,
        ),
        input_output_aliases={} if new_weight is None else {5: 0},
        compiler_params=pltpu.CompilerParams(vmem_limit_bytes=60 << 20),
        cost_estimate=cost(2 * down, width, 5),
        name="precondition_home",
    )(kept_column, roots, grad, roots, weight, *extra)


def finish_columns(flags, down, across, q, col_count, new_weight, piece, tokens, start, width, later_than):
    depth = piece.shape[0]
    at = (q * piece.shape[1] + start) // width
    height = depth // down
    rows = tokens.shape[0] // col_count
    half = col_count // 2
    tile = min(width, 256)

    def kernel(flag_ref, weight_ref, piece_ref, token_ref, *rest):
        new_ref, others_ref, mine_ref = rest[-3:]
        step = pl.program_id(0)

        @pl.when(step == 0)
        def _():
            for p in range(down):
                own = slice(p * height, (p + 1) * height)

                @pl.when(flag_ref[p * across + q] != 0)
                def _():
                    new_ref[own, :] = weight_ref[own, :]

                @pl.when(flag_ref[p * across + q] == 0)
                def _():
                    update = step_size * piece_ref[own, :].astype(jnp.float32)
                    new_ref[own, :] = (weight_ref[own, :].astype(jnp.float32) - update).astype(jnp.bfloat16)

        def product(out_ref):
            @pl.loop(0, width // tile)
            def _(i):
                some = pl.ds(pl.multiple_of(i * tile, tile), tile)
                term = jnp.dot(token_ref[...], new_ref[:, some], preferred_element_type=jnp.float32)
                out_ref[:, some] = term.astype(jnp.bfloat16)

        @pl.when(step < half)
        def _():
            product(others_ref)

        @pl.when(step >= half)
        def _():
            product(mine_ref)

    def chunk(t, f):
        core = f[down * across]
        return jnp.where(t < half, 2 * t + 1 - core, 2 * (t - half) + core)

    columns = pl.BlockSpec((depth, width), lambda t, f: (0, at))
    terms = jax.ShapeDtypeStruct((half, rows, width), jnp.bfloat16)
    return pl.pallas_call(
        kernel,
        out_shape=(jax.ShapeDtypeStruct(new_weight.shape, jnp.bfloat16), terms, terms),
        grid_spec=pltpu.PrefetchScalarGridSpec(
            num_scalar_prefetch=1,
            grid=(col_count,),
            in_specs=[
                columns,
                pl.BlockSpec((depth, width), lambda t, f: (0, start // width)),
                pl.BlockSpec((rows, depth), lambda t, f: (chunk(t, f), 0)),
            ]
            + [pl.BlockSpec(memory_space=pl.ANY)] * len(later_than),
            out_specs=(
                columns,
                pl.BlockSpec((None, rows, width), lambda t, f: (jnp.minimum(t, half - 1), 0, 0)),
                pl.BlockSpec((None, rows, width), lambda t, f: (jnp.maximum(t - half, 0), 0, 0)),
            ),
        ),
        input_output_aliases={1: 0},
        compiler_params=pltpu.CompilerParams(vmem_limit_bytes=56 << 20),
        cost_estimate=pl.CostEstimate(flops=1000, bytes_accessed=1000, transcendentals=0),
        name="finish_columns",
    )(flags, new_weight, piece, tokens, *later_than)


def swap_tokens(tokens, row_count, row_place):
    other = lax.ppermute(tokens, "row", pair_route(row_count))
    low = jnp.mod(row_place, 2) == 0
    return jnp.concatenate([jnp.where(low, tokens, other), jnp.where(low, other, tokens)], axis=0)


def ring_direct(pair, row_count, side):
    sides = range(side, row_count, 2)
    return [
        lax.ppermute(pair, "row", [(i, (i + 2 * step) % row_count) for i in sides])
        for step in range(1, row_count // 2)
    ]


def line_step(up, down, row_count, side):
    ups = lax.ppermute(up, "row", [(i, i + 2) for i in range(side, row_count - 2, 2)])
    downs = lax.ppermute(down, "row", [(i + 2, i) for i in range(side, row_count - 2, 2)])
    return ups, downs


def put_pairs(pair, early, late, row_place):
    pairs = len(early) + 1
    rows, depth = pair.shape
    ups = [up for up, _ in late]
    downs = [below for _, below in late]

    def kernel(place_ref, *refs):
        pair_ref, *others, out_ref, sem = refs
        early_refs, up_refs, down_refs = (others[i * (pairs - 1):(i + 1) * (pairs - 1)] for i in range(3))
        t = pl.program_id(0)
        apart = place_ref[0] - t
        odd = place_ref[1] == 1
        cases = [(apart == 0, pair_ref)]
        for step in range(1, pairs):
            cases.append((jnp.logical_and(odd, apart == step), up_refs[step - 1]))
            cases.append((jnp.logical_and(odd, apart == -step), down_refs[step - 1]))
            around = jnp.logical_or(apart == step, apart == step - pairs)
            cases.append((jnp.logical_and(jnp.logical_not(odd), around), early_refs[step - 1]))
        for case, source in cases:
            @pl.when(case)
            def _():
                copy = pltpu.make_async_copy(source, out_ref, sem)
                copy.start()
                copy.wait()

    count = 1 + 3 * (pairs - 1)
    return pl.pallas_call(
        kernel,
        out_shape=jax.ShapeDtypeStruct((rows * pairs, depth), pair.dtype),
        grid_spec=pltpu.PrefetchScalarGridSpec(
            num_scalar_prefetch=1,
            grid=(pairs,),
            in_specs=[pl.BlockSpec(memory_space=pl.ANY)] * count,
            out_specs=pl.BlockSpec((rows, depth), lambda t, f: (t, 0)),
            scratch_shapes=[pltpu.SemaphoreType.DMA],
        ),
        cost_estimate=pl.CostEstimate(flops=1000, bytes_accessed=1000, transcendentals=0),
        name="put_pairs",
    )(jnp.stack([row_place // 2, row_place % 2]), pair, *early, *ups, *downs)


def far_sum(mine, came, col_count, col_place):
    halves = mine.astype(jnp.float32) + came.astype(jnp.float32)
    groups = col_count // 2
    place = col_place // 2
    total = lax.dynamic_index_in_dim(halves, place, 0, keepdims=False)
    sent = halves.astype(jnp.bfloat16)
    for step in range(1, groups):
        piece = lax.dynamic_index_in_dim(sent, jnp.mod(place + step, groups), 0, keepdims=False)
        total = total + lax.ppermute(piece, "col", shift_route(col_count, 2 * step)).astype(jnp.float32)
    return total.astype(jnp.bfloat16)


def on_device(tokens, weight, grad, roots, owner):
    width = roots.shape[-1]
    down = weight.shape[0] // width
    across = weight.shape[1] // width
    row_place = lax.axis_index("row")
    col_place = lax.axis_index("col")
    row_count = lax.axis_size("row")
    col_count = lax.axis_size("col")
    previous = jnp.mod(row_place - 1 + row_count, row_count)
    own_owner = lax.dynamic_slice(owner, (col_place * down, row_place * across), (down, across))
    prior_owner = lax.dynamic_slice(owner, (col_place * down, previous * across), (down, across))
    kept = (own_owner == row_place).astype(jnp.int32)
    taken = (prior_owner == row_place).astype(jnp.int32)
    forth = shift_route(row_count, 1)
    back = shift_route(row_count, -1)

    swapped = swap_tokens(tokens, row_count, row_place)
    swapped, grad = together(swapped, grad)
    came = lax.ppermute(grad, "row", forth)
    early = ring_direct(swapped, row_count, 0)
    new_weight = precondition_home(kept[:, 0], roots, grad, weight, 0, None, ())
    came, late_pair, new_weight, *early = together(came, swapped, new_weight, *early)

    returned = []
    up, down_piece = line_step(late_pair, late_pair, row_count, 1)
    late = [(up, down_piece)]
    returned = []
    later_than = ()
    for q in range(across):
        lent, mark = precondition_lent(taken[:, q], roots, q, came, (0, width), later_than)
        returned.append(lax.ppermute(lent, "row", back))
        later_than = (mark,)
        if q > 0:
            new_weight = precondition_home(kept[:, q], roots, grad, weight, q, new_weight, later_than)

    for step in range(2, row_count // 2):
        if step == row_count // 2 - 1:
            up, down_piece, new_weight = together(up, down_piece, new_weight)
        up, down_piece = line_step(up, down_piece, row_count, 1)
        late.append((up, down_piece))
    all_tokens = put_pairs(swapped, early, late, row_place)
    output = jnp.zeros((all_tokens.shape[0] // col_count, weight.shape[1]), jnp.bfloat16)

    flags = jnp.concatenate([kept.reshape(-1), jnp.mod(col_place, 2).reshape(1)])

    half = width // 2
    parts = [(q, 0, width) for q in range(across - 1)] + [(across - 1, 0, half), (across - 1, half, half)]
    later_than = ()
    ahead = ()
    for k, (q, start, size) in enumerate(parts):
        if k == len(parts) - 1:
            later_than = later_than + ahead
        new_weight, others, mine = finish_columns(
            flags, down, across, q, col_count, new_weight, returned[q], all_tokens, start, size, later_than
        )
        other = lax.ppermute(others, "col", pair_route(col_count))
        total = far_sum(mine, other, col_count, col_place)
        output = lax.dynamic_update_slice(output, total, (0, q * width + start))
        later_than = (mine,)
        if q < across - 1:
            ahead = ahead + (total,)
    return new_weight, output


def solution(mesh):
    placed = (
        P("row", "col"),
        P("col", "row"),
        P("col", "row"),
        P(None, "col", None, "row", None, None),
        P(),
    )
    return jax.shard_map(
        on_device,
        mesh=mesh,
        in_specs=placed,
        out_specs=(P("col", "row"), P("col", "row")),
        check_vma=False,
    )
```

```python
import jax
import jax.numpy as jnp
from jax import lax
from jax.experimental import pallas as pl
from jax.experimental.pallas import tpu as pltpu
from jax.sharding import PartitionSpec as P

step_size = 0.5


def shift_route(count, distance):
    return [(i, (i + distance) % count) for i in range(count)]


def pair_route(count):
    return [(i, i ^ 1) for i in range(count)]


def together(*values):
    return lax.optimization_barrier(values)


def root_spec(roots, side, slot, block):
    width = roots.shape[-1]
    return pl.BlockSpec((None, None, None, None, width, width), lambda *at: (side, block(*at)[0], slot, block(*at)[1], 0, 0))


def update_rows(left_ref, grad_ref, right_ref, rows):
    mixed = jnp.dot(left_ref[rows, :], grad_ref[...], preferred_element_type=jnp.float32)
    return jnp.dot(mixed.astype(jnp.bfloat16), right_ref[...], preferred_element_type=jnp.float32)


def cost(blocks, width, arrays):
    return pl.CostEstimate(
        flops=blocks * 4 * width**3, bytes_accessed=blocks * 2 * arrays * width * width, transcendentals=0
    )


def precondition_lent(flags, roots, q, came, cuts, later_than):
    width = roots.shape[-1]
    down = came.shape[0] // width
    tile = min(width, 256)
    pieces = list(zip(cuts[:-1], cuts[1:]))

    def kernel(flag_ref, left_ref, grad_ref, right_ref, *rest):
        *out_refs, mark_ref = rest[-len(pieces) - 1:]
        mark_ref[...] = jnp.zeros_like(mark_ref)

        @pl.when(flag_ref[pl.program_id(0)] != 0)
        def _():
            @pl.loop(0, width // tile)
            def _(i):
                rows = pl.ds(pl.multiple_of(i * tile, tile), tile)
                update = update_rows(left_ref, grad_ref, right_ref, rows).astype(jnp.bfloat16)
                for (start, stop), out_ref in zip(pieces, out_refs):
                    out_ref[rows, :] = update[:, start:stop]

        @pl.when(flag_ref[pl.program_id(0)] == 0)
        def _():
            for out_ref in out_refs:
                out_ref[...] = jnp.zeros_like(out_ref)

    return pl.pallas_call(
        kernel,
        out_shape=[jax.ShapeDtypeStruct((down * width, stop - start), jnp.bfloat16) for start, stop in pieces]
        + [jax.ShapeDtypeStruct((8, 128), jnp.float32)],
        grid_spec=pltpu.PrefetchScalarGridSpec(
            num_scalar_prefetch=1,
            grid=(down,),
            in_specs=[
                root_spec(roots, 0, 1, lambda p, f: (p, q)),
                pl.BlockSpec((width, width), lambda p, f: (p, 0)),
                root_spec(roots, 1, 1, lambda p, f: (p, q)),
            ]
            + [pl.BlockSpec(memory_space=pl.ANY)] * len(later_than),
            out_specs=[pl.BlockSpec((width, stop - start), lambda p, f: (p, 0)) for start, stop in pieces]
            + [pl.BlockSpec((8, 128), lambda p, f: (0, 0))],
        ),
        compiler_params=pltpu.CompilerParams(vmem_limit_bytes=60 << 20),
        cost_estimate=cost(down, width, 4),
        name="precondition_lent",
    )(flags, roots, came, roots, *later_than)


def precondition_home(kept_column, roots, grad, weight, q, new_weight, later_than):
    width = roots.shape[-1]
    down = kept_column.shape[0]
    tile = min(width, 256)

    def kernel(flag_ref, left_ref, grad_ref, right_ref, weight_ref, *rest):
        out_ref = rest[-1]

        @pl.when(flag_ref[pl.program_id(0)] != 0)
        def _():
            @pl.loop(0, width // tile)
            def _(i):
                rows = pl.ds(pl.multiple_of(i * tile, tile), tile)
                update = update_rows(left_ref, grad_ref, right_ref, rows)
                out_ref[rows, :] = (weight_ref[rows, :].astype(jnp.float32) - step_size * update).astype(jnp.bfloat16)

        @pl.when(flag_ref[pl.program_id(0)] == 0)
        def _():
            out_ref[...] = weight_ref[...]

    tiles = pl.BlockSpec((width, width), lambda p, f: (p, q))
    extra = ([] if new_weight is None else [new_weight]) + list(later_than)
    return pl.pallas_call(
        kernel,
        out_shape=jax.ShapeDtypeStruct(weight.shape, jnp.bfloat16),
        grid_spec=pltpu.PrefetchScalarGridSpec(
            num_scalar_prefetch=1,
            grid=(down,),
            in_specs=[
                root_spec(roots, 0, 0, lambda p, f: (p, q)),
                tiles,
                root_spec(roots, 1, 0, lambda p, f: (p, q)),
                tiles,
            ]
            + [pl.BlockSpec(memory_space=pl.ANY)] * len(extra),
            out_specs=tiles,
        ),
        input_output_aliases={} if new_weight is None else {5: 0},
        compiler_params=pltpu.CompilerParams(vmem_limit_bytes=60 << 20),
        cost_estimate=cost(4 * down, width, 5),
        name="precondition_home",
    )(kept_column, roots, grad, roots, weight, *extra)


def finish_columns(flags, down, across, q, col_count, new_weight, piece, tokens, start, width, later_than):
    depth = piece.shape[0]
    at = (q * piece.shape[1] + start) // width
    height = depth // down
    rows = tokens.shape[0] // col_count
    half = col_count // 2
    tile = min(width, 256)

    def kernel(flag_ref, weight_ref, piece_ref, token_ref, *rest):
        new_ref, others_ref, mine_ref = rest[-3:]
        step = pl.program_id(0)

        @pl.when(step == 0)
        def _():
            for p in range(down):
                own = slice(p * height, (p + 1) * height)

                @pl.when(flag_ref[p * across + q] != 0)
                def _():
                    new_ref[own, :] = weight_ref[own, :]

                @pl.when(flag_ref[p * across + q] == 0)
                def _():
                    update = step_size * piece_ref[own, :].astype(jnp.float32)
                    new_ref[own, :] = (weight_ref[own, :].astype(jnp.float32) - update).astype(jnp.bfloat16)

        def product(out_ref):
            @pl.loop(0, width // tile)
            def _(i):
                some = pl.ds(pl.multiple_of(i * tile, tile), tile)
                term = jnp.dot(token_ref[...], new_ref[:, some], preferred_element_type=jnp.float32)
                out_ref[:, some] = term.astype(jnp.bfloat16)

        @pl.when(step < half)
        def _():
            product(others_ref)

        @pl.when(step >= half)
        def _():
            product(mine_ref)

    def chunk(t, f):
        core = f[down * across]
        return jnp.where(t < half, 2 * t + 1 - core, 2 * (t - half) + core)

    columns = pl.BlockSpec((depth, width), lambda t, f: (0, at))
    terms = jax.ShapeDtypeStruct((half, rows, width), jnp.bfloat16)
    return pl.pallas_call(
        kernel,
        out_shape=(jax.ShapeDtypeStruct(new_weight.shape, jnp.bfloat16), terms, terms),
        grid_spec=pltpu.PrefetchScalarGridSpec(
            num_scalar_prefetch=1,
            grid=(col_count,),
            in_specs=[
                columns,
                pl.BlockSpec((depth, width), lambda t, f: (0, start // width)),
                pl.BlockSpec((rows, depth), lambda t, f: (chunk(t, f), 0)),
            ]
            + [pl.BlockSpec(memory_space=pl.ANY)] * len(later_than),
            out_specs=(
                columns,
                pl.BlockSpec((None, rows, width), lambda t, f: (jnp.minimum(t, half - 1), 0, 0)),
                pl.BlockSpec((None, rows, width), lambda t, f: (jnp.maximum(t - half, 0), 0, 0)),
            ),
        ),
        input_output_aliases={1: 0},
        compiler_params=pltpu.CompilerParams(vmem_limit_bytes=56 << 20),
        cost_estimate=pl.CostEstimate(flops=1000, bytes_accessed=1000, transcendentals=0),
        name="finish_columns",
    )(flags, new_weight, piece, tokens, *later_than)


def swap_tokens(tokens, row_count, row_place):
    other = lax.ppermute(tokens, "row", pair_route(row_count))
    low = jnp.mod(row_place, 2) == 0
    return jnp.concatenate([jnp.where(low, tokens, other), jnp.where(low, other, tokens)], axis=0)


def ring_direct(pair, row_count, side):
    sides = range(side, row_count, 2)
    return [
        lax.ppermute(pair, "row", [(i, (i + 2 * step) % row_count) for i in sides])
        for step in range(1, row_count // 2)
    ]


def line_step(up, down, row_count, side):
    ups = lax.ppermute(up, "row", [(i, i + 2) for i in range(side, row_count - 2, 2)])
    downs = lax.ppermute(down, "row", [(i + 2, i) for i in range(side, row_count - 2, 2)])
    return ups, downs


def put_pairs(pair, early, late, row_place):
    pairs = len(early) + 1
    rows, depth = pair.shape
    ups = [up for up, _ in late]
    downs = [below for _, below in late]

    def kernel(place_ref, *refs):
        pair_ref, *others, out_ref, sem = refs
        early_refs, up_refs, down_refs = (others[i * (pairs - 1):(i + 1) * (pairs - 1)] for i in range(3))
        t = pl.program_id(0)
        apart = place_ref[0] - t
        odd = place_ref[1] == 1
        cases = [(apart == 0, pair_ref)]
        for step in range(1, pairs):
            cases.append((jnp.logical_and(odd, apart == step), up_refs[step - 1]))
            cases.append((jnp.logical_and(odd, apart == -step), down_refs[step - 1]))
            around = jnp.logical_or(apart == step, apart == step - pairs)
            cases.append((jnp.logical_and(jnp.logical_not(odd), around), early_refs[step - 1]))
        for case, source in cases:
            @pl.when(case)
            def _():
                copy = pltpu.make_async_copy(source, out_ref, sem)
                copy.start()
                copy.wait()

    count = 1 + 3 * (pairs - 1)
    return pl.pallas_call(
        kernel,
        out_shape=jax.ShapeDtypeStruct((rows * pairs, depth), pair.dtype),
        grid_spec=pltpu.PrefetchScalarGridSpec(
            num_scalar_prefetch=1,
            grid=(pairs,),
            in_specs=[pl.BlockSpec(memory_space=pl.ANY)] * count,
            out_specs=pl.BlockSpec((rows, depth), lambda t, f: (t, 0)),
            scratch_shapes=[pltpu.SemaphoreType.DMA],
        ),
        cost_estimate=pl.CostEstimate(flops=1000, bytes_accessed=1000, transcendentals=0),
        name="put_pairs",
    )(jnp.stack([row_place // 2, row_place % 2]), pair, *early, *ups, *downs)


def far_sum(mine, came, col_count, col_place):
    halves = mine.astype(jnp.float32) + came.astype(jnp.float32)
    groups = col_count // 2
    place = col_place // 2
    total = lax.dynamic_index_in_dim(halves, place, 0, keepdims=False)
    sent = halves.astype(jnp.bfloat16)
    for step in range(1, groups):
        piece = lax.dynamic_index_in_dim(sent, jnp.mod(place + step, groups), 0, keepdims=False)
        total = total + lax.ppermute(piece, "col", shift_route(col_count, 2 * step)).astype(jnp.float32)
    return total.astype(jnp.bfloat16)


def on_device(tokens, weight, grad, roots, owner):
    width = roots.shape[-1]
    down = weight.shape[0] // width
    across = weight.shape[1] // width
    row_place = lax.axis_index("row")
    col_place = lax.axis_index("col")
    row_count = lax.axis_size("row")
    col_count = lax.axis_size("col")
    previous = jnp.mod(row_place - 1 + row_count, row_count)
    own_owner = lax.dynamic_slice(owner, (col_place * down, row_place * across), (down, across))
    prior_owner = lax.dynamic_slice(owner, (col_place * down, previous * across), (down, across))
    kept = (own_owner == row_place).astype(jnp.int32)
    taken = (prior_owner == row_place).astype(jnp.int32)
    forth = shift_route(row_count, 1)
    back = shift_route(row_count, -1)

    swapped = swap_tokens(tokens, row_count, row_place)
    columns = [grad[:, q * width:(q + 1) * width] for q in range(across)]
    swapped, *columns = together(swapped, *columns)
    came = [lax.ppermute(column, "row", forth) for column in columns]
    early = ring_direct(swapped, row_count, 0)
    lents = []
    later_than = ()
    for q in range(across - 1):
        lent, mark = precondition_lent(taken[:, q], roots, q, came[q], (0, width), later_than)
        lents.append(lent)
        later_than = (mark,)
    new_weight = precondition_home(kept[:, 0], roots, grad, weight, 0, None, later_than)
    last, late_pair, new_weight, *rest = together(came[-1], swapped, new_weight, *lents, *early)
    lents, early = rest[:across - 1], rest[across - 1:]

    returned = [lax.ppermute(lent, "row", back) for lent in lents]
    up, down_piece = line_step(late_pair, late_pair, row_count, 1)
    late = [(up, down_piece)]
    lent, mark = precondition_lent(taken[:, across - 1], roots, across - 1, last, (0, width), ())
    returned.append(lax.ppermute(lent, "row", back))
    for q in range(1, across):
        new_weight = precondition_home(kept[:, q], roots, grad, weight, q, new_weight, (mark,))

    for step in range(2, row_count // 2):
        if step == row_count // 2 - 1:
            up, down_piece, new_weight = together(up, down_piece, new_weight)
        up, down_piece = line_step(up, down_piece, row_count, 1)
        late.append((up, down_piece))
    all_tokens = put_pairs(swapped, early, late, row_place)
    output = jnp.zeros((all_tokens.shape[0] // col_count, weight.shape[1]), jnp.bfloat16)

    flags = jnp.concatenate([kept.reshape(-1), jnp.mod(col_place, 2).reshape(1)])

    half = width // 2
    parts = [(q, 0, width) for q in range(across - 1)] + [(across - 1, 0, half), (across - 1, half, half)]
    later_than = ()
    ahead = ()
    for k, (q, start, size) in enumerate(parts):
        if k == len(parts) - 1:
            later_than = later_than + ahead
        new_weight, others, mine = finish_columns(
            flags, down, across, q, col_count, new_weight, returned[q], all_tokens, start, size, later_than
        )
        other = lax.ppermute(others, "col", pair_route(col_count))
        total = far_sum(mine, other, col_count, col_place)
        output = lax.dynamic_update_slice(output, total, (0, q * width + start))
        later_than = (mine,)
        if q < across - 1:
            ahead = ahead + (total,)
    return new_weight, output


def solution(mesh):
    placed = (
        P("row", "col"),
        P("col", "row"),
        P("col", "row"),
        P(None, "col", None, "row", None, None),
        P(),
    )
    return jax.shard_map(
        on_device,
        mesh=mesh,
        in_specs=placed,
        out_specs=(P("col", "row"), P("col", "row")),
        check_vma=False,
    )
```

```python
import jax
import jax.numpy as jnp
from jax import lax
from jax.experimental import pallas as pl
from jax.experimental.pallas import tpu as pltpu
from jax.sharding import PartitionSpec as P

step_size = 0.5


def shift_route(count, distance):
    return [(i, (i + distance) % count) for i in range(count)]


def pair_route(count):
    return [(i, i ^ 1) for i in range(count)]


def together(*values):
    return lax.optimization_barrier(values)


def root_spec(roots, side, slot, block):
    width = roots.shape[-1]
    return pl.BlockSpec((None, None, None, None, width, width), lambda *at: (side, block(*at)[0], slot, block(*at)[1], 0, 0))


def update_rows(left_ref, grad_ref, right_ref, rows):
    mixed = jnp.dot(left_ref[rows, :], grad_ref[...], preferred_element_type=jnp.float32)
    return jnp.dot(mixed.astype(jnp.bfloat16), right_ref[...], preferred_element_type=jnp.float32)


def cost(blocks, width, arrays):
    return pl.CostEstimate(
        flops=blocks * 4 * width**3, bytes_accessed=blocks * 2 * arrays * width * width, transcendentals=0
    )


def precondition_lent(flags, roots, q, came, cuts, later_than):
    width = roots.shape[-1]
    down = came.shape[0] // width
    tile = min(width, 256)
    pieces = list(zip(cuts[:-1], cuts[1:]))

    def kernel(flag_ref, left_ref, grad_ref, right_ref, *rest):
        *out_refs, mark_ref = rest[-len(pieces) - 1:]
        mark_ref[...] = jnp.zeros_like(mark_ref)

        @pl.when(flag_ref[pl.program_id(0)] != 0)
        def _():
            @pl.loop(0, width // tile)
            def _(i):
                rows = pl.ds(pl.multiple_of(i * tile, tile), tile)
                update = update_rows(left_ref, grad_ref, right_ref, rows).astype(jnp.bfloat16)
                for (start, stop), out_ref in zip(pieces, out_refs):
                    out_ref[rows, :] = update[:, start:stop]

        @pl.when(flag_ref[pl.program_id(0)] == 0)
        def _():
            for out_ref in out_refs:
                out_ref[...] = jnp.zeros_like(out_ref)

    return pl.pallas_call(
        kernel,
        out_shape=[jax.ShapeDtypeStruct((down * width, stop - start), jnp.bfloat16) for start, stop in pieces]
        + [jax.ShapeDtypeStruct((8, 128), jnp.float32)],
        grid_spec=pltpu.PrefetchScalarGridSpec(
            num_scalar_prefetch=1,
            grid=(down,),
            in_specs=[
                root_spec(roots, 0, 1, lambda p, f: (p, q)),
                pl.BlockSpec((width, width), lambda p, f: (p, 0)),
                root_spec(roots, 1, 1, lambda p, f: (p, q)),
            ]
            + [pl.BlockSpec(memory_space=pl.ANY)] * len(later_than),
            out_specs=[pl.BlockSpec((width, stop - start), lambda p, f: (p, 0)) for start, stop in pieces]
            + [pl.BlockSpec((8, 128), lambda p, f: (0, 0))],
        ),
        compiler_params=pltpu.CompilerParams(vmem_limit_bytes=60 << 20),
        cost_estimate=cost(down, width, 4),
        name="precondition_lent",
    )(flags, roots, came, roots, *later_than)


def precondition_home(kept_column, roots, grad, weight, q, new_weight, later_than):
    width = roots.shape[-1]
    down = kept_column.shape[0]
    tile = min(width, 256)

    def kernel(flag_ref, left_ref, grad_ref, right_ref, weight_ref, *rest):
        out_ref = rest[-1]

        @pl.when(flag_ref[pl.program_id(0)] != 0)
        def _():
            @pl.loop(0, width // tile)
            def _(i):
                rows = pl.ds(pl.multiple_of(i * tile, tile), tile)
                update = update_rows(left_ref, grad_ref, right_ref, rows)
                out_ref[rows, :] = (weight_ref[rows, :].astype(jnp.float32) - step_size * update).astype(jnp.bfloat16)

        @pl.when(flag_ref[pl.program_id(0)] == 0)
        def _():
            out_ref[...] = weight_ref[...]

    tiles = pl.BlockSpec((width, width), lambda p, f: (p, q))
    extra = ([] if new_weight is None else [new_weight]) + list(later_than)
    return pl.pallas_call(
        kernel,
        out_shape=jax.ShapeDtypeStruct(weight.shape, jnp.bfloat16),
        grid_spec=pltpu.PrefetchScalarGridSpec(
            num_scalar_prefetch=1,
            grid=(down,),
            in_specs=[
                root_spec(roots, 0, 0, lambda p, f: (p, q)),
                tiles,
                root_spec(roots, 1, 0, lambda p, f: (p, q)),
                tiles,
            ]
            + [pl.BlockSpec(memory_space=pl.ANY)] * len(extra),
            out_specs=tiles,
        ),
        input_output_aliases={} if new_weight is None else {5: 0},
        compiler_params=pltpu.CompilerParams(vmem_limit_bytes=60 << 20),
        cost_estimate=cost(4 * down, width, 5),
        name="precondition_home",
    )(kept_column, roots, grad, roots, weight, *extra)


def finish_columns(flags, down, across, q, col_count, new_weight, piece, tokens, start, width, later_than):
    depth = piece.shape[0]
    at = (q * piece.shape[1] + start) // width
    height = depth // down
    rows = tokens.shape[0] // col_count
    half = col_count // 2
    tile = min(width, 256)

    def kernel(flag_ref, weight_ref, piece_ref, token_ref, *rest):
        new_ref, others_ref, mine_ref = rest[-3:]
        step = pl.program_id(0)

        @pl.when(step == 0)
        def _():
            for p in range(down):
                own = slice(p * height, (p + 1) * height)

                @pl.when(flag_ref[p * across + q] != 0)
                def _():
                    new_ref[own, :] = weight_ref[own, :]

                @pl.when(flag_ref[p * across + q] == 0)
                def _():
                    update = step_size * piece_ref[own, :].astype(jnp.float32)
                    new_ref[own, :] = (weight_ref[own, :].astype(jnp.float32) - update).astype(jnp.bfloat16)

        def product(out_ref):
            @pl.loop(0, width // tile)
            def _(i):
                some = pl.ds(pl.multiple_of(i * tile, tile), tile)
                term = jnp.dot(token_ref[...], new_ref[:, some], preferred_element_type=jnp.float32)
                out_ref[:, some] = term.astype(jnp.bfloat16)

        @pl.when(step < half)
        def _():
            product(others_ref)

        @pl.when(step >= half)
        def _():
            product(mine_ref)

    def chunk(t, f):
        core = f[down * across]
        return jnp.where(t < half, 2 * t + 1 - core, 2 * (t - half) + core)

    columns = pl.BlockSpec((depth, width), lambda t, f: (0, at))
    terms = jax.ShapeDtypeStruct((half, rows, width), jnp.bfloat16)
    return pl.pallas_call(
        kernel,
        out_shape=(jax.ShapeDtypeStruct(new_weight.shape, jnp.bfloat16), terms, terms),
        grid_spec=pltpu.PrefetchScalarGridSpec(
            num_scalar_prefetch=1,
            grid=(col_count,),
            in_specs=[
                columns,
                pl.BlockSpec((depth, width), lambda t, f: (0, start // width)),
                pl.BlockSpec((rows, depth), lambda t, f: (chunk(t, f), 0)),
            ]
            + [pl.BlockSpec(memory_space=pl.ANY)] * len(later_than),
            out_specs=(
                columns,
                pl.BlockSpec((None, rows, width), lambda t, f: (jnp.minimum(t, half - 1), 0, 0)),
                pl.BlockSpec((None, rows, width), lambda t, f: (jnp.maximum(t - half, 0), 0, 0)),
            ),
        ),
        input_output_aliases={1: 0},
        compiler_params=pltpu.CompilerParams(vmem_limit_bytes=56 << 20),
        cost_estimate=pl.CostEstimate(flops=1000, bytes_accessed=1000, transcendentals=0),
        name="finish_columns",
    )(flags, new_weight, piece, tokens, *later_than)


def swap_tokens(tokens, row_count, row_place):
    other = lax.ppermute(tokens, "row", pair_route(row_count))
    low = jnp.mod(row_place, 2) == 0
    return jnp.concatenate([jnp.where(low, tokens, other), jnp.where(low, other, tokens)], axis=0)


def ring_direct(pair, row_count, side):
    sides = range(side, row_count, 2)
    return [
        lax.ppermute(pair, "row", [(i, (i + 2 * step) % row_count) for i in sides])
        for step in range(1, row_count // 2)
    ]


def line_step(up, down, row_count, side):
    ups = lax.ppermute(up, "row", [(i, i + 2) for i in range(side, row_count - 2, 2)])
    downs = lax.ppermute(down, "row", [(i + 2, i) for i in range(side, row_count - 2, 2)])
    return ups, downs


def put_pairs(pair, early, late, row_place):
    pairs = len(early) + 1
    rows, depth = pair.shape
    ups = [up for up, _ in late]
    downs = [below for _, below in late]

    def kernel(place_ref, *refs):
        pair_ref, *others, out_ref, sem = refs
        early_refs, up_refs, down_refs = (others[i * (pairs - 1):(i + 1) * (pairs - 1)] for i in range(3))
        t = pl.program_id(0)
        apart = place_ref[0] - t
        odd = place_ref[1] == 1
        cases = [(apart == 0, pair_ref)]
        for step in range(1, pairs):
            cases.append((jnp.logical_and(odd, apart == step), up_refs[step - 1]))
            cases.append((jnp.logical_and(odd, apart == -step), down_refs[step - 1]))
            around = jnp.logical_or(apart == step, apart == step - pairs)
            cases.append((jnp.logical_and(jnp.logical_not(odd), around), early_refs[step - 1]))
        for case, source in cases:
            @pl.when(case)
            def _():
                copy = pltpu.make_async_copy(source, out_ref, sem)
                copy.start()
                copy.wait()

    count = 1 + 3 * (pairs - 1)
    return pl.pallas_call(
        kernel,
        out_shape=jax.ShapeDtypeStruct((rows * pairs, depth), pair.dtype),
        grid_spec=pltpu.PrefetchScalarGridSpec(
            num_scalar_prefetch=1,
            grid=(pairs,),
            in_specs=[pl.BlockSpec(memory_space=pl.ANY)] * count,
            out_specs=pl.BlockSpec((rows, depth), lambda t, f: (t, 0)),
            scratch_shapes=[pltpu.SemaphoreType.DMA],
        ),
        cost_estimate=pl.CostEstimate(flops=1000, bytes_accessed=1000, transcendentals=0),
        name="put_pairs",
    )(jnp.stack([row_place // 2, row_place % 2]), pair, *early, *ups, *downs)


def far_sum(mine, came, col_count, col_place):
    groups = col_count // 2
    place = col_place // 2

    def half(index):
        both = [lax.dynamic_index_in_dim(x, index, 0, keepdims=False).astype(jnp.float32) for x in (mine, came)]
        return both[0] + both[1]

    arrived = []
    for step in range(1, groups):
        piece = half(jnp.mod(place + step, groups)).astype(jnp.bfloat16)
        arrived.append(lax.ppermute(piece, "col", shift_route(col_count, 2 * step)))
    total = half(place)
    for piece in arrived:
        total = total + piece.astype(jnp.float32)
    return total.astype(jnp.bfloat16), arrived


def on_device(tokens, weight, grad, roots, owner):
    width = roots.shape[-1]
    down = weight.shape[0] // width
    across = weight.shape[1] // width
    row_place = lax.axis_index("row")
    col_place = lax.axis_index("col")
    row_count = lax.axis_size("row")
    col_count = lax.axis_size("col")
    previous = jnp.mod(row_place - 1 + row_count, row_count)
    own_owner = lax.dynamic_slice(owner, (col_place * down, row_place * across), (down, across))
    prior_owner = lax.dynamic_slice(owner, (col_place * down, previous * across), (down, across))
    kept = (own_owner == row_place).astype(jnp.int32)
    taken = (prior_owner == row_place).astype(jnp.int32)
    forth = shift_route(row_count, 1)
    back = shift_route(row_count, -1)

    swapped = swap_tokens(tokens, row_count, row_place)
    columns = [grad[:, q * width:(q + 1) * width] for q in range(across)]
    swapped, *columns = together(swapped, *columns)
    came = [lax.ppermute(column, "row", forth) for column in columns]
    early = ring_direct(swapped, row_count, 0)
    lents = []
    later_than = ()
    for q in range(across - 1):
        lent, mark = precondition_lent(taken[:, q], roots, q, came[q], (0, width), later_than)
        lents.append(lent)
        later_than = (mark,)
    new_weight = precondition_home(kept[:, 0], roots, grad, weight, 0, None, later_than)
    last, late_pair, new_weight, *rest = together(came[-1], swapped, new_weight, *lents, *early)
    lents, early = rest[:across - 1], rest[across - 1:]

    returned = [lax.ppermute(lent, "row", back) for lent in lents]
    up, down_piece = line_step(late_pair, late_pair, row_count, 1)
    late = [(up, down_piece)]
    lent, mark = precondition_lent(taken[:, across - 1], roots, across - 1, last, (0, width), ())
    returned.append(lax.ppermute(lent, "row", back))
    for q in range(1, across):
        new_weight = precondition_home(kept[:, q], roots, grad, weight, q, new_weight, (mark,))

    for step in range(2, row_count // 2):
        if step == row_count // 2 - 1:
            up, down_piece, new_weight = together(up, down_piece, new_weight)
        up, down_piece = line_step(up, down_piece, row_count, 1)
        late.append((up, down_piece))
    all_tokens = put_pairs(swapped, early, late, row_place)
    output = jnp.zeros((all_tokens.shape[0] // col_count, weight.shape[1]), jnp.bfloat16)

    flags = jnp.concatenate([kept.reshape(-1), jnp.mod(col_place, 2).reshape(1)])

    half = width // 2
    parts = [(q, 0, width) for q in range(across - 1)] + [(across - 1, 0, half), (across - 1, half, half)]
    later_than = ()
    ahead = ()
    for k, (q, start, size) in enumerate(parts):
        if k == len(parts) - 1:
            later_than = later_than + ahead
        new_weight, others, mine = finish_columns(
            flags, down, across, q, col_count, new_weight, returned[q], all_tokens, start, size, later_than
        )
        other = lax.ppermute(others, "col", pair_route(col_count))
        total, arrived = far_sum(mine, other, col_count, col_place)
        output = lax.dynamic_update_slice(output, total, (0, q * width + start))
        later_than = (mine,)
        if q < across - 1:
            ahead = ahead + tuple(arrived)
    return new_weight, output


def solution(mesh):
    placed = (
        P("row", "col"),
        P("col", "row"),
        P("col", "row"),
        P(None, "col", None, "row", None, None),
        P(),
    )
    return jax.shard_map(
        on_device,
        mesh=mesh,
        in_specs=placed,
        out_specs=(P("col", "row"), P("col", "row")),
        check_vma=False,
    )
```

```python
import jax
import jax.numpy as jnp
from jax import lax
from jax.experimental import pallas as pl
from jax.experimental.pallas import tpu as pltpu
from jax.sharding import PartitionSpec as P

step_size = 0.5


def shift_route(count, distance):
    return [(i, (i + distance) % count) for i in range(count)]


def pair_route(count):
    return [(i, i ^ 1) for i in range(count)]


def together(*values):
    return lax.optimization_barrier(values)


def root_spec(roots, side, slot, block):
    width = roots.shape[-1]
    return pl.BlockSpec((None, None, None, None, width, width), lambda *at: (side, block(*at)[0], slot, block(*at)[1], 0, 0))


def update_rows(left_ref, grad_ref, right_ref, rows):
    mixed = jnp.dot(left_ref[rows, :], grad_ref[...], preferred_element_type=jnp.float32)
    return jnp.dot(mixed.astype(jnp.bfloat16), right_ref[...], preferred_element_type=jnp.float32)


def cost(blocks, width, arrays):
    return pl.CostEstimate(
        flops=blocks * 4 * width**3, bytes_accessed=blocks * 2 * arrays * width * width, transcendentals=0
    )


def precondition_lent(flags, roots, q, came, cuts, later_than):
    width = roots.shape[-1]
    down = came.shape[0] // width
    tile = min(width, 256)
    pieces = list(zip(cuts[:-1], cuts[1:]))

    def kernel(flag_ref, left_ref, grad_ref, right_ref, *rest):
        *out_refs, mark_ref = rest[-len(pieces) - 1:]
        mark_ref[...] = jnp.zeros_like(mark_ref)

        @pl.when(flag_ref[pl.program_id(0)] != 0)
        def _():
            @pl.loop(0, width // tile)
            def _(i):
                rows = pl.ds(pl.multiple_of(i * tile, tile), tile)
                update = update_rows(left_ref, grad_ref, right_ref, rows).astype(jnp.bfloat16)
                for (start, stop), out_ref in zip(pieces, out_refs):
                    out_ref[rows, :] = update[:, start:stop]

        @pl.when(flag_ref[pl.program_id(0)] == 0)
        def _():
            for out_ref in out_refs:
                out_ref[...] = jnp.zeros_like(out_ref)

    return pl.pallas_call(
        kernel,
        out_shape=[jax.ShapeDtypeStruct((down * width, stop - start), jnp.bfloat16) for start, stop in pieces]
        + [jax.ShapeDtypeStruct((8, 128), jnp.float32)],
        grid_spec=pltpu.PrefetchScalarGridSpec(
            num_scalar_prefetch=1,
            grid=(down,),
            in_specs=[
                root_spec(roots, 0, 1, lambda p, f: (p, q)),
                pl.BlockSpec((width, width), lambda p, f: (p, 0)),
                root_spec(roots, 1, 1, lambda p, f: (p, q)),
            ]
            + [pl.BlockSpec(memory_space=pl.ANY)] * len(later_than),
            out_specs=[pl.BlockSpec((width, stop - start), lambda p, f: (p, 0)) for start, stop in pieces]
            + [pl.BlockSpec((8, 128), lambda p, f: (0, 0))],
        ),
        compiler_params=pltpu.CompilerParams(vmem_limit_bytes=60 << 20),
        cost_estimate=cost(down, width, 4),
        name="precondition_lent",
    )(flags, roots, came, roots, *later_than)


def precondition_home(kept_column, roots, grad, weight, q, new_weight, later_than):
    width = roots.shape[-1]
    down = kept_column.shape[0]
    tile = min(width, 256)

    def kernel(flag_ref, left_ref, grad_ref, right_ref, weight_ref, *rest):
        out_ref = rest[-1]

        @pl.when(flag_ref[pl.program_id(0)] != 0)
        def _():
            @pl.loop(0, width // tile)
            def _(i):
                rows = pl.ds(pl.multiple_of(i * tile, tile), tile)
                update = update_rows(left_ref, grad_ref, right_ref, rows)
                out_ref[rows, :] = (weight_ref[rows, :].astype(jnp.float32) - step_size * update).astype(jnp.bfloat16)

        @pl.when(flag_ref[pl.program_id(0)] == 0)
        def _():
            out_ref[...] = weight_ref[...]

    tiles = pl.BlockSpec((width, width), lambda p, f: (p, q))
    extra = ([] if new_weight is None else [new_weight]) + list(later_than)
    return pl.pallas_call(
        kernel,
        out_shape=jax.ShapeDtypeStruct(weight.shape, jnp.bfloat16),
        grid_spec=pltpu.PrefetchScalarGridSpec(
            num_scalar_prefetch=1,
            grid=(down,),
            in_specs=[
                root_spec(roots, 0, 0, lambda p, f: (p, q)),
                tiles,
                root_spec(roots, 1, 0, lambda p, f: (p, q)),
                tiles,
            ]
            + [pl.BlockSpec(memory_space=pl.ANY)] * len(extra),
            out_specs=tiles,
        ),
        input_output_aliases={} if new_weight is None else {5: 0},
        compiler_params=pltpu.CompilerParams(vmem_limit_bytes=60 << 20),
        cost_estimate=cost(4 * down, width, 5),
        name="precondition_home",
    )(kept_column, roots, grad, roots, weight, *extra)


def finish_columns(flags, down, across, q, col_count, new_weight, piece, tokens, start, width, later_than):
    depth = piece.shape[0]
    at = (q * piece.shape[1] + start) // width
    height = depth // down
    rows = tokens.shape[0] // col_count
    half = col_count // 2
    tile = min(width, 256)

    def kernel(flag_ref, weight_ref, piece_ref, token_ref, *rest):
        new_ref, others_ref, mine_ref = rest[-3:]
        step = pl.program_id(0)

        @pl.when(step == 0)
        def _():
            for p in range(down):
                own = slice(p * height, (p + 1) * height)

                @pl.when(flag_ref[p * across + q] != 0)
                def _():
                    new_ref[own, :] = weight_ref[own, :]

                @pl.when(flag_ref[p * across + q] == 0)
                def _():
                    update = step_size * piece_ref[own, :].astype(jnp.float32)
                    new_ref[own, :] = (weight_ref[own, :].astype(jnp.float32) - update).astype(jnp.bfloat16)

        def product(out_ref):
            @pl.loop(0, width // tile)
            def _(i):
                some = pl.ds(pl.multiple_of(i * tile, tile), tile)
                term = jnp.dot(token_ref[...], new_ref[:, some], preferred_element_type=jnp.float32)
                out_ref[:, some] = term.astype(jnp.bfloat16)

        @pl.when(step < half)
        def _():
            product(others_ref)

        @pl.when(step >= half)
        def _():
            product(mine_ref)

    def chunk(t, f):
        core = f[down * across]
        return jnp.where(t < half, 2 * t + 1 - core, 2 * (t - half) + core)

    columns = pl.BlockSpec((depth, width), lambda t, f: (0, at))
    terms = jax.ShapeDtypeStruct((half, rows, width), jnp.bfloat16)
    return pl.pallas_call(
        kernel,
        out_shape=(jax.ShapeDtypeStruct(new_weight.shape, jnp.bfloat16), terms, terms),
        grid_spec=pltpu.PrefetchScalarGridSpec(
            num_scalar_prefetch=1,
            grid=(col_count,),
            in_specs=[
                columns,
                pl.BlockSpec((depth, width), lambda t, f: (0, start // width)),
                pl.BlockSpec((rows, depth), lambda t, f: (chunk(t, f), 0)),
            ]
            + [pl.BlockSpec(memory_space=pl.ANY)] * len(later_than),
            out_specs=(
                columns,
                pl.BlockSpec((None, rows, width), lambda t, f: (jnp.minimum(t, half - 1), 0, 0)),
                pl.BlockSpec((None, rows, width), lambda t, f: (jnp.maximum(t - half, 0), 0, 0)),
            ),
        ),
        input_output_aliases={1: 0},
        compiler_params=pltpu.CompilerParams(vmem_limit_bytes=56 << 20),
        cost_estimate=pl.CostEstimate(flops=1000, bytes_accessed=1000, transcendentals=0),
        name="finish_columns",
    )(flags, new_weight, piece, tokens, *later_than)


def swap_tokens(tokens, row_count, row_place):
    other = lax.ppermute(tokens, "row", pair_route(row_count))
    low = jnp.mod(row_place, 2) == 0
    return jnp.concatenate([jnp.where(low, tokens, other), jnp.where(low, other, tokens)], axis=0)


def ring_direct(pair, row_count, side):
    sides = range(side, row_count, 2)
    return [
        lax.ppermute(pair, "row", [(i, (i + 2 * step) % row_count) for i in sides])
        for step in range(1, row_count // 2)
    ]


def line_step(up, down, row_count, side):
    ups = lax.ppermute(up, "row", [(i, i + 2) for i in range(side, row_count - 2, 2)])
    downs = lax.ppermute(down, "row", [(i + 2, i) for i in range(side, row_count - 2, 2)])
    return ups, downs


def put_pairs(pair, early, late, row_place):
    pairs = len(early) + 1
    rows, depth = pair.shape
    ups = [up for up, _ in late]
    downs = [below for _, below in late]

    def kernel(place_ref, *refs):
        pair_ref, *others, out_ref, sems = refs
        early_refs, up_refs, down_refs = (others[i * (pairs - 1):(i + 1) * (pairs - 1)] for i in range(3))
        odd = place_ref[1] == 1
        copies = []
        for t in range(pairs):
            apart = place_ref[0] - t
            cases = [(apart == 0, pair_ref)]
            for step in range(1, pairs):
                cases.append((jnp.logical_and(odd, apart == step), up_refs[step - 1]))
                cases.append((jnp.logical_and(odd, apart == -step), down_refs[step - 1]))
                around = jnp.logical_or(apart == step, apart == step - pairs)
                cases.append((jnp.logical_and(jnp.logical_not(odd), around), early_refs[step - 1]))
            for case, source in cases:
                copies.append((case, source, out_ref.at[pl.ds(t * rows, rows), :], sems.at[t]))
        for case, *copy in copies:
            pl.when(case)(lambda copy=copy: pltpu.make_async_copy(*copy).start())
        for case, *copy in copies:
            pl.when(case)(lambda copy=copy: pltpu.make_async_copy(*copy).wait())

    count = 1 + 3 * (pairs - 1)
    return pl.pallas_call(
        kernel,
        out_shape=jax.ShapeDtypeStruct((rows * pairs, depth), pair.dtype),
        grid_spec=pltpu.PrefetchScalarGridSpec(
            num_scalar_prefetch=1,
            grid=(1,),
            in_specs=[pl.BlockSpec(memory_space=pl.ANY)] * count,
            out_specs=pl.BlockSpec((rows * pairs, depth), lambda t, f: (0, 0)),
            scratch_shapes=[pltpu.SemaphoreType.DMA((pairs,))],
        ),
        compiler_params=pltpu.CompilerParams(vmem_limit_bytes=40 << 20),
        cost_estimate=pl.CostEstimate(flops=1000, bytes_accessed=1000, transcendentals=0),
        name="put_pairs",
    )(jnp.stack([row_place // 2, row_place % 2]), pair, *early, *ups, *downs)


def far_sum(mine, came, col_count, col_place):
    groups = col_count // 2
    place = col_place // 2

    def half(index):
        both = [lax.dynamic_index_in_dim(x, index, 0, keepdims=False).astype(jnp.float32) for x in (mine, came)]
        return both[0] + both[1]

    arrived = []
    for step in range(1, groups):
        piece = half(jnp.mod(place + step, groups)).astype(jnp.bfloat16)
        arrived.append(lax.ppermute(piece, "col", shift_route(col_count, 2 * step)))
    total = half(place)
    for piece in arrived:
        total = total + piece.astype(jnp.float32)
    return total.astype(jnp.bfloat16), arrived


def on_device(tokens, weight, grad, roots, owner):
    width = roots.shape[-1]
    down = weight.shape[0] // width
    across = weight.shape[1] // width
    row_place = lax.axis_index("row")
    col_place = lax.axis_index("col")
    row_count = lax.axis_size("row")
    col_count = lax.axis_size("col")
    previous = jnp.mod(row_place - 1 + row_count, row_count)
    own_owner = lax.dynamic_slice(owner, (col_place * down, row_place * across), (down, across))
    prior_owner = lax.dynamic_slice(owner, (col_place * down, previous * across), (down, across))
    kept = (own_owner == row_place).astype(jnp.int32)
    taken = (prior_owner == row_place).astype(jnp.int32)
    forth = shift_route(row_count, 1)
    back = shift_route(row_count, -1)

    swapped = swap_tokens(tokens, row_count, row_place)
    columns = [grad[:, q * width:(q + 1) * width] for q in range(across)]
    swapped, *columns = together(swapped, *columns)
    came = [lax.ppermute(column, "row", forth) for column in columns]
    early = ring_direct(swapped, row_count, 0)
    lents = []
    later_than = ()
    for q in range(across - 1):
        lent, mark = precondition_lent(taken[:, q], roots, q, came[q], (0, width), later_than)
        lents.append(lent)
        later_than = (mark,)
    new_weight = precondition_home(kept[:, 0], roots, grad, weight, 0, None, later_than)
    last, late_pair, new_weight, *rest = together(came[-1], swapped, new_weight, *lents, *early)
    lents, early = rest[:across - 1], rest[across - 1:]

    returned = [lax.ppermute(lent, "row", back) for lent in lents]
    up, down_piece = line_step(late_pair, late_pair, row_count, 1)
    late = [(up, down_piece)]
    lent, mark = precondition_lent(taken[:, across - 1], roots, across - 1, last, (0, width), ())
    returned.append(lax.ppermute(lent, "row", back))
    for q in range(1, across):
        new_weight = precondition_home(kept[:, q], roots, grad, weight, q, new_weight, (mark,))

    for step in range(2, row_count // 2):
        if step == row_count // 2 - 1:
            up, down_piece, new_weight = together(up, down_piece, new_weight)
        up, down_piece = line_step(up, down_piece, row_count, 1)
        late.append((up, down_piece))
    all_tokens = put_pairs(swapped, early, late, row_place)
    output = jnp.zeros((all_tokens.shape[0] // col_count, weight.shape[1]), jnp.bfloat16)

    flags = jnp.concatenate([kept.reshape(-1), jnp.mod(col_place, 2).reshape(1)])

    half = width // 2
    parts = [(q, 0, width) for q in range(across - 1)] + [(across - 1, 0, half), (across - 1, half, half)]
    later_than = ()
    ahead = ()
    for k, (q, start, size) in enumerate(parts):
        if k == len(parts) - 1:
            later_than = later_than + ahead
        new_weight, others, mine = finish_columns(
            flags, down, across, q, col_count, new_weight, returned[q], all_tokens, start, size, later_than
        )
        other = lax.ppermute(others, "col", pair_route(col_count))
        total, arrived = far_sum(mine, other, col_count, col_place)
        output = lax.dynamic_update_slice(output, total, (0, q * width + start))
        later_than = (mine,)
        if q < across - 1:
            ahead = ahead + tuple(arrived)
    return new_weight, output


def solution(mesh):
    placed = (
        P("row", "col"),
        P("col", "row"),
        P("col", "row"),
        P(None, "col", None, "row", None, None),
        P(),
    )
    return jax.shard_map(
        on_device,
        mesh=mesh,
        in_specs=placed,
        out_specs=(P("col", "row"), P("col", "row")),
        check_vma=False,
    )
```
